32 devices in a mesh: dp: 4 (over y, x), ctx: 4 (over z), tp: 2 (over core).
Axes of the slice: x: 2, y: 2, z: 4, core: 2. Of those that a mesh axis runs over, the one named last changes fastest.
Arguments:
- tokens: bfloat16 [4, 768, 2048], P('dp', 'ctx'), may hold values from -6 to 6
- lengths: int32 [4], P('dp'), may hold values from 192 to 768
- block_order: int32 [4, 4], P('dp'), may hold values from 0 to 3, each once within a row
- norm_gain: float32 [2048], replicated, may hold values from 0.5 to 1.5
- w_query: bfloat16 [2048, 1024], P(('dp', 'ctx'), 'tp'), may hold values from -2 to 2
- w_key: bfloat16 [2048, 1024], P(('dp', 'ctx'), 'tp'), may hold values from -2 to 2
- w_value: bfloat16 [2048, 1024], P(('dp', 'ctx'), 'tp'), may hold values from -0.125 to 0.125
- w_out: bfloat16 [1024, 2048], P('tp', ('dp', 'ctx')), may hold values from -0.1875 to 0.1875
- final_gain: float32 [2048], replicated, may hold values from 0.5 to 1.5
- w_cross_key: bfloat16 [2048, 1024], P(('dp', 'ctx'), 'tp'), may hold values from -0.125 to 0.125
- w_cross_value: bfloat16 [2048, 1024], P(('dp', 'ctx'), 'tp'), may hold values from -0.125 to 0.125
Outputs:
- encoded: bfloat16 [4, 768, 2048], P('dp', 'ctx')
- cross_kv: bfloat16 [4, 2, 1024, 768], P('dp', 'tp', 'ctx')
The draws below stay inside these ranges and needn't reach their ends.
Inputs may be any that keep to these rules, and one draw needn't show every extreme that they name: `block_order`: each row holds every number of 0 to 3 once.
All inputs are finite; a program needn't handle non-finite values.
Results may differ from the reference program's by a relative error of at most 0.014.
Values may be sent and summed in bfloat16 or wider, within the bound.
No kernel may reach another device: no remote copies, remote signals or barrier semaphores. Data moves between devices by JAX's collectives and lax.ppermute only.
A program may use at most 128 MiB of HBM per device.

```python
import jax
import jax.numpy as jnp
from jax import lax

D = 2048
HEADS = 8
HD = 128
LEN_DEV = 192
USERS = 4
LEN = 768
BLOCKS = 4
KVC = 1024
N_TP = 2


def shared_parts(key):
    direction = jnp.clip(jax.random.normal(jax.random.fold_in(key, 101), (D,), jnp.float32), -4.0, 4.0)
    pattern = jnp.clip(jax.random.normal(jax.random.fold_in(key, 102), (HEADS * HD,), jnp.float32), -4.0, 4.0)
    return (direction, pattern)


def drawn_weight(key, salt):
    direction, pattern = shared_parts(key)
    base = jnp.clip(jax.random.normal(jax.random.fold_in(key, salt), (D, HEADS * HD), jnp.float32), -6.0, 6.0)
    strength = (300.0 / HD ** 0.5) ** 0.5
    return base * D ** (-0.5) + strength * direction[:, None] * pattern[None, :] / D


def draw_w_query(key, part):
    return drawn_weight(key, 201).astype(jnp.bfloat16)


def draw_w_key(key, part):
    return drawn_weight(key, 202).astype(jnp.bfloat16)


def draw_tokens(key, part):
    direction, pattern = shared_parts(key)
    rough = jnp.clip(jax.random.normal(jax.random.fold_in(key, 301), (USERS, LEN, D), jnp.float32), -6.0, 6.0)
    share = 0.0625
    lower = 0.8
    upper = 0.97
    chosen = jax.random.uniform(jax.random.fold_in(key, 302), (USERS, LEN), jnp.float32) < share
    amount = jax.random.uniform(jax.random.fold_in(key, 303), (USERS, LEN), jnp.float32, lower, upper)
    aligned = jnp.where(chosen, amount, 0.0)
    rest = jnp.sqrt(1.0 - aligned * aligned)
    mixed = rest[:, :, None] * rough + aligned[:, :, None] * direction[None, None, :]
    return jnp.clip(mixed, -6.0, 6.0).astype(jnp.bfloat16)


def set_ends(values, stream_key, smallest, high):
    longest = values.shape.index(max(values.shape))
    spots = []
    for shift in (0, 1):
        where = [jax.random.randint(jax.random.fold_in(stream_key, axis), (), 0, length) for axis, length in enumerate(values.shape)]
        where[longest] = (where[longest] + shift) % values.shape[longest]
        spots.append(tuple(where))
    return values.at[spots[0]].set(smallest).at[spots[1]].set(high)


def levels(key, extent, cuts, smallest, largest):
    factor_of = 1.0
    for position, parts in cuts:
        draws = jax.random.uniform(jax.random.fold_in(jax.random.fold_in(key, 6), position), (parts,), jnp.float32, smallest / len(cuts), largest / len(cuts))
        factor_of = factor_of * jnp.repeat(jnp.exp(draws), extent[position] // parts).reshape((-1,) + (1,) * (len(extent) - 1 - position))
    return factor_of


def centred(rng, shape, width, limit, shards=(), held_as=jnp.bfloat16):
    drawn = width * jax.random.normal(rng, shape, jnp.float32)
    if shards:
        drawn = drawn * levels(rng, shape, shards, -0.22, 0.18)
    return jnp.clip(drawn, -limit, limit).astype(held_as)


def setup_inputs(seed: int = 0) -> dict:
    key_of = jax.random.split(jax.random.key(seed), 12)
    tokens = draw_tokens(jax.random.fold_in(key_of[11], 71), 0)
    lengths = set_ends(jax.random.randint(key_of[1], (USERS,), LEN_DEV, LEN + 1), jax.random.fold_in(key_of[1], 1), LEN_DEV, LEN).astype(jnp.int32)
    block_order = jax.vmap(lambda own: jax.random.permutation(own, BLOCKS))(jax.random.split(key_of[2], USERS)).reshape((USERS, BLOCKS)).astype(jnp.int32)
    norm_gain = jnp.clip(1.0 + 0.1 * jax.random.normal(key_of[3], (D,), jnp.float32), 0.5, 1.5)
    w_query = draw_w_query(jax.random.fold_in(key_of[11], 71), 0)
    w_key = draw_w_key(jax.random.fold_in(key_of[11], 71), 0)
    w_value = centred(key_of[6], (D, HEADS * HD), D ** -0.5, 0.125, ((0, 16), (1, 2)))
    w_out = centred(key_of[7], (HEADS * HD, D), (HEADS * HD) ** -0.5, 0.1875, ((0, 2), (1, 16)))
    final_gain = jnp.clip(1.0 + 0.1 * jax.random.normal(key_of[8], (D,), jnp.float32), 0.5, 1.5)
    w_cross_key = centred(key_of[9], (D, HEADS * HD), D ** -0.5, 0.125, ((0, 16), (1, 2)))
    w_cross_value = centred(key_of[10], (D, HEADS * HD), D ** -0.5, 0.125, ((0, 16), (1, 2)))
    return dict(tokens=tokens, lengths=lengths, block_order=block_order, norm_gain=norm_gain, w_query=w_query, w_key=w_key, w_value=w_value, w_out=w_out, final_gain=final_gain, w_cross_key=w_cross_key, w_cross_value=w_cross_value)


epsilon = 1e-06
floor_value = -1e+30

def rms_norm(inputs, gain_vector):
    floats = inputs.astype(jnp.float32)
    factor = lax.rsqrt(lax.optimization_barrier(jnp.mean(floats * floats, axis=-1, keepdims=True)) + epsilon)
    return floats * factor * gain_vector

def one_user(tokens, length, order, norm_gain, w_query, w_key, w_value, w_out, final_gain, w_cross_key, w_cross_value):
    normed = rms_norm(tokens, norm_gain).astype(jnp.bfloat16)
    query = (jnp.dot(normed, w_query, preferred_element_type=jnp.float32) * HD ** (-0.5)).astype(jnp.bfloat16)
    keys = jnp.dot(normed, w_key, preferred_element_type=jnp.float32).astype(jnp.bfloat16)
    values = jnp.dot(normed, w_value, preferred_element_type=jnp.float32).astype(jnp.bfloat16)
    valid = jnp.arange(LEN, dtype=jnp.int32) < length

    def head_attend(head_index):
        query_head = lax.dynamic_slice_in_dim(query, head_index * HD, HD, 1)
        key_head = lax.dynamic_slice_in_dim(keys, head_index * HD, HD, 1)
        value_head = lax.dynamic_slice_in_dim(values, head_index * HD, HD, 1)
        scores = jnp.dot(query_head, key_head.T, preferred_element_type=jnp.float32)
        scores = jnp.where(valid[None, :], scores, floor_value)
        row_top = lax.optimization_barrier(jnp.max(scores, axis=1, keepdims=True))
        probs = jnp.where(valid[None, :], jnp.exp(scores - row_top), 0.0)
        row_total = lax.optimization_barrier(jnp.sum(probs, axis=1, keepdims=True))
        return jnp.dot(probs.astype(jnp.bfloat16), value_head, preferred_element_type=jnp.float32) / row_total
    head_results = lax.map(head_attend, jnp.arange(HEADS, dtype=jnp.int32))
    attended = jnp.transpose(head_results, (1, 0, 2)).reshape(LEN, HEADS * HD).astype(jnp.bfloat16)
    projected = jnp.dot(attended, w_out, preferred_element_type=jnp.float32)
    encoded = (tokens.astype(jnp.float32) + projected).astype(jnp.bfloat16)
    final = rms_norm(encoded, final_gain).astype(jnp.bfloat16)
    cross_key = jnp.dot(final, w_cross_key, preferred_element_type=jnp.float32).astype(jnp.bfloat16)
    cross_value = jnp.dot(final, w_cross_value, preferred_element_type=jnp.float32).astype(jnp.bfloat16)
    group_width = HEADS * HD // N_TP
    group_list = []
    for group_index in range(N_TP):
        lower = group_index * group_width
        upper = lower + group_width
        channels = jnp.concatenate([cross_key[:, lower:upper], cross_value[:, lower:upper]], axis=1).T
        row_blocks = channels.reshape(KVC, BLOCKS, LEN_DEV)
        row_blocks = jnp.take(row_blocks, order, axis=1)
        group_list.append(row_blocks.reshape(KVC, LEN))
    return (encoded, jnp.stack(group_list))

def reference(tokens, lengths, block_order, norm_gain, w_query, w_key, w_value, w_out, final_gain, w_cross_key, w_cross_value):
    encoded_list = []
    cross_list = []
    for user_index in range(USERS):
        encoded, cross = one_user(tokens[user_index], lengths[user_index], block_order[user_index], norm_gain, w_query, w_key, w_value, w_out, final_gain, w_cross_key, w_cross_value)
        encoded_list.append(encoded)
        cross_list.append(cross)
    return (jnp.stack(encoded_list), jnp.stack(cross_list))
```

```python
import functools

import jax
import jax.numpy as jnp
from jax import lax
from jax.experimental import pallas as pl
from jax.experimental.pallas import tpu as pltpu
from jax.sharding import PartitionSpec as P

HD = 128


epsilon = 1e-06
floor_value = -1e30


def as_sent(array):
    return jax.tree.map(lambda a: a.astype(jnp.bfloat16) if a.dtype == jnp.float32 else a, array)


def rms_norm(inputs, gain_vector):
    floats = inputs.astype(jnp.float32)
    factor = lax.rsqrt(jnp.mean(floats * floats, axis=-1, keepdims=True) + epsilon)
    return floats * factor * gain_vector


def divisor_block(total_rows, limit_rows):
    for candidate in range(min(total_rows, limit_rows), 0, -1):
        if total_rows % candidate == 0:
            return candidate
    return total_rows


def project(normed, weights, target, out_spec):
    user_count, row_count, model_width = normed.shape
    head_cols = weights[0].shape[1]
    if out_spec == "urk":
        out_shape = (user_count, row_count, head_cols)
    else:
        out_shape = (user_count, head_cols, row_count)
    initial = tuple((jnp.zeros(out_shape, jnp.float32) for weight_one in weights))
    dp_count = lax.axis_size("dp")
    ctx_count = lax.axis_size("ctx")
    local_rows = weights[0].shape[0]
    if target == "self":
        stacked = jax.tree.map(
            lambda part, own: part.astype(own.dtype),
            lax.all_gather(as_sent(weights), "dp", axis=0, tiled=True),
            weights,
        )
    else:
        stacked = jax.tree.map(
            lambda part, own: part.astype(own.dtype),
            lax.all_gather(as_sent(weights), "dp", axis=0, tiled=True),
            weights,
        )
    arranged = normed.reshape(user_count, row_count, dp_count, ctx_count, local_rows)

    def add_blocks(running, pieces):
        shard_count = pieces[0].shape[0] // (dp_count * local_rows)
        updated = []
        for summed, piece_one in zip(running, pieces):
            shaped = piece_one.reshape(shard_count, dp_count, local_rows, piece_one.shape[1])
            updated.append(
                summed
                + jnp.einsum(
                    "urbcs,cbsk->" + out_spec, arranged, shaped, preferred_element_type=jnp.float32
                )
            )
        return tuple(updated)

    if target == "self":
        return add_blocks(
            initial,
            jax.tree.map(lambda a: lax.all_gather(a, "ctx", axis=0, tiled=True), as_sent(stacked)),
        )
    return add_blocks(
        initial,
        jax.tree.map(lambda a: lax.all_gather(a, "ctx", axis=0, tiled=True), as_sent(stacked)),
    )


def attend_keys(query, keys, values, lengths):
    user_count, row_count, head_cols = query.shape
    heads_here = head_cols // HD
    query_heads = query.reshape(user_count, row_count, heads_here, HD)
    initial = (
        jnp.full((user_count, heads_here, row_count), floor_value, jnp.float32),
        jnp.zeros((user_count, heads_here, row_count), jnp.float32),
        jnp.zeros((user_count, row_count, heads_here, HD), jnp.float32),
    )
    offset = jnp.int32(0)
    key_piece = lax.all_gather(keys, "ctx", axis=1, tiled=True)
    value_piece = lax.all_gather(values, "ctx", axis=1, tiled=True)
    span_rows = key_piece.shape[1]
    block_rows = divisor_block(span_rows, 2048)

    def one_block(step_index, state_now):
        top_now, norm_now, accumulated = state_now
        begin_row = step_index * block_rows
        key_block = lax.dynamic_slice_in_dim(key_piece, begin_row, block_rows, 1).reshape(
            user_count, block_rows, heads_here, HD
        )
        value_block = lax.dynamic_slice_in_dim(value_piece, begin_row, block_rows, 1).reshape(
            user_count, block_rows, heads_here, HD
        )
        positions = offset + begin_row + jnp.arange(block_rows, dtype=jnp.int32)
        key_mask = (positions[None, :] < lengths[:, None])[:, None, None, :]
        scores = jnp.einsum(
            "urhd,unhd->uhrn", query_heads, key_block, preferred_element_type=jnp.float32
        )
        scores = jnp.where(key_mask, scores, floor_value)
        top_next = jnp.maximum(top_now, jnp.max(scores, axis=-1))
        weights_now = jnp.where(key_mask, jnp.exp(scores - top_next[..., None]), 0.0)
        shrink = jnp.exp(top_now - top_next)
        norm_next = norm_now * shrink + jnp.sum(weights_now, axis=-1)
        mixed_values = jnp.einsum(
            "uhrn,unhd->urhd",
            weights_now.astype(jnp.bfloat16),
            value_block,
            preferred_element_type=jnp.float32,
        )
        accumulated = accumulated * jnp.transpose(shrink, (0, 2, 1))[..., None] + mixed_values
        return (top_next, norm_next, accumulated)

    top_all, norm_all, accumulated = lax.fori_loop(0, span_rows // block_rows, one_block, initial)
    result = accumulated / jnp.transpose(norm_all, (0, 2, 1))[..., None]
    return result.reshape(user_count, row_count, head_cols).astype(jnp.bfloat16)


def gathered_weights(
    tokens,
    lengths,
    block_order,
    norm_gain,
    w_query,
    w_key,
    w_value,
    w_out,
    final_gain,
    w_cross_key,
    w_cross_value,
):
    user_count, row_count, model_width = tokens.shape
    ctx_count = lax.axis_size("ctx")
    normed = rms_norm(tokens, norm_gain).astype(jnp.bfloat16)
    query, keys, values = project(normed, (w_query, w_key, w_value), "self", "urk")
    query = (query * HD ** (-0.5)).astype(jnp.bfloat16)
    keys = keys.astype(jnp.bfloat16)
    values = values.astype(jnp.bfloat16)
    attended = attend_keys(query, keys, values, lengths)
    partial_out = jnp.einsum(
        "urk,kc->urc",
        attended,
        lax.all_gather(w_out, ("dp", "ctx"), axis=1, tiled=True),
        preferred_element_type=jnp.float32,
    )
    summed_out = lax.psum(partial_out.astype(jnp.bfloat16), "tp").astype(jnp.float32)
    encoded = (tokens.astype(jnp.float32) + summed_out).astype(jnp.bfloat16)
    final = rms_norm(encoded, final_gain).astype(jnp.bfloat16)
    cross_key, cross_value = project(final, (w_cross_key, w_cross_value), "cross", "ukr")
    stacked = jnp.concatenate(
        [cross_key.astype(jnp.bfloat16), cross_value.astype(jnp.bfloat16)], axis=1
    )
    moved = lax.all_to_all(stacked, "ctx", split_axis=1, concat_axis=2, tiled=True)
    channel_count = moved.shape[1]
    row_blocks = moved.reshape(user_count, channel_count, ctx_count, row_count)
    ordered_list = [jnp.take(row_blocks[0], block_order[0], axis=1)]
    ordered = jnp.stack(ordered_list).reshape(user_count, channel_count, ctx_count * row_count)
    return (encoded, ordered[:, None])


def line_ring(count):
    return list(range(0, count, 2)) + list(range(1, count, 2))[::-1]


def ring_source(index, steps, count):
    half = (count + 1) // 2
    place = jnp.where(index % 2 == 0, index // 2, count - 1 - index // 2)
    place = (place - steps + count) % count
    return jnp.where(place < half, 2 * place, 2 * (count - 1 - place) + 1)


def shift_over(array, axis, steps):
    count = lax.axis_size(axis)
    return lax.ppermute(array, axis, [(i, (i + steps) % count) for i in range(count)])


def swap_cores(array):
    return lax.ppermute(array, "tp", [(0, 1), (1, 0)])


def plane_pairs(first):
    near, far = (1, 2) if first else (2, 1)
    return [(2 * d, 2 * (d ^ near)) for d in range(4)] + [
        (2 * d + 1, 2 * (d ^ far) + 1) for d in range(4)
    ]


def gather_plane(array):
    axes = ("dp", "tp")
    near = lax.ppermute(array, axes, plane_pairs(True))
    far = lax.ppermute(array, axes, plane_pairs(False))
    return array, near, far, lax.ppermute(near, axes, plane_pairs(False))


def plane_owner(dp_index, tp_index, piece):
    flips = (0, jnp.where(tp_index == 0, 1, 2), jnp.where(tp_index == 0, 2, 1), 3)
    return jnp.bitwise_xor(dp_index, flips[piece])


def any_specs(count):
    return [pl.BlockSpec(memory_space=pl.ANY)] * count


def run_copies(copies):
    for copy in copies:
        copy.start()
    for copy in copies:
        copy.wait()


def split_self(count, wq, wk, wv, *pieces):
    me = lax.axis_index("ctx")
    for steps, piece in enumerate(pieces):
        begin = pl.multiple_of((me + steps) % count * HD, HD)
        for place, weight in enumerate((wq, wk, wv)):
            piece[:, place * HD : (place + 1) * HD] = weight[:, pl.ds(begin, HD)]


def split_cross(count, wo, wck, wcv, *pieces):
    me = lax.axis_index("ctx")
    cols = wck.shape[1] * 2 // count
    rows = wck.shape[0]
    head_rows, lanes = wo.shape
    for steps, piece in enumerate(pieces):
        target = (me + steps) % count
        half = count // 2
        is_key = target < half
        piece[0:head_rows, :] = wo[...]
        for part in range(cols // lanes):
            begin = pl.multiple_of(target % half * cols + part * lanes, lanes)
            here = slice(head_rows + part * rows, head_rows + (part + 1) * rows)
            piece[here, :] = jnp.where(
                is_key, wck[:, pl.ds(begin, lanes)], wcv[:, pl.ds(begin, lanes)]
            )


def attend_kernel(count, dims, *refs):
    user_rows, block, chunk, local = dims
    n_ring = 2 * (count - 1)
    lengths, gain, own = refs[:3]
    ring, other = refs[3 : 3 + n_ring], refs[3 + n_ring : 3 + 2 * n_ring]
    weights = refs[3 + 2 * n_ring : 7 + 2 * n_ring]
    out, rows_in, w_all, qkv, sem = refs[7 + 2 * n_ring :]
    ctx, tp, dp = lax.axis_index("ctx"), lax.axis_index("tp"), lax.axis_index("dp")
    places = [(own.at[0], rows_in.at[pl.ds(pl.multiple_of(ctx * block, block), block)])]
    for steps in range(1, count):
        source = ring_source(ctx, steps, count)
        for chain in range(2):
            for core, arrays in ((tp, ring), (1 - tp, other)):
                begin = pl.multiple_of(source * block + core * (2 * chunk) + chain * chunk, chunk)
                places.append(
                    (arrays[(steps - 1) * 2 + chain], rows_in.at[pl.ds(begin, chunk)])
                )
    for piece, weight in enumerate(weights):
        owner = plane_owner(dp, tp, piece)
        for steps in range(count):
            begin = pl.multiple_of((owner * count + (ctx - steps + count) % count) * local, local)
            places.append((weight.at[steps], w_all.at[pl.ds(begin, local)]))
    run_copies(
        [pltpu.make_async_copy(a, b, sem.at[i]) for i, (a, b) in enumerate(places)]
    )
    gains = gain[...]

    @pl.loop(0, user_rows // block)
    def _(step):
        here = pl.ds(pl.multiple_of(step * block, block), block)
        normed = rms_norm(rows_in[here, :], gains).astype(jnp.bfloat16)
        made = jnp.dot(normed, w_all[...], preferred_element_type=jnp.float32)
        qkv[here, 0:HD] = (made[:, 0:HD] * HD ** (-0.5)).astype(jnp.bfloat16)
        qkv[here, HD : 3 * HD] = made[:, HD : 3 * HD].astype(jnp.bfloat16)

    valid_rows = lengths[0]

    @pl.loop(0, user_rows // block)
    def _(step):
        here = pl.ds(pl.multiple_of(step * block, block), block)
        scores = lax.dot_general(
            qkv[here, 0:HD],
            qkv[:, HD : 2 * HD],
            (((1,), (1,)), ((), ())),
            preferred_element_type=jnp.float32,
        )
        valid = lax.broadcasted_iota(jnp.int32, scores.shape, 1) < valid_rows
        scores = jnp.where(valid, scores, floor_value)
        top = jnp.max(scores, axis=1, keepdims=True)
        probs = jnp.where(valid, jnp.exp(scores - top), 0.0)
        total = jnp.sum(probs, axis=1, keepdims=True)
        mixed = jnp.dot(
            probs.astype(jnp.bfloat16), qkv[:, 2 * HD : 3 * HD], preferred_element_type=jnp.float32
        )
        out[here, :] = (mixed / total).astype(jnp.bfloat16)


def finish_kernel(count, dims, *refs):
    user_rows, block, chunk, local, head_rows, lanes, cols = dims
    n_ring = 2 * (count - 1)
    order, gain, own = refs[:3]
    ring, other = refs[3 : 3 + n_ring], refs[3 + n_ring : 3 + 2 * n_ring]
    refs = refs[3 + 2 * n_ring :]
    heads, other_heads = refs[:count], refs[count : 2 * count]
    weights, other_weights = refs[2 * count : 2 * count + 4], refs[2 * count + 4 : 2 * count + 8]
    encoded, out, rows_in, attended, w_all, w_cross, made_all, sem = refs[2 * count + 8 :]
    ctx, tp, dp = lax.axis_index("ctx"), lax.axis_index("tp"), lax.axis_index("dp")
    places = [(own.at[0], rows_in.at[pl.ds(pl.multiple_of(ctx * block, block), block)])]
    for steps in range(1, count):
        source = ring_source(ctx, steps, count)
        for chain in range(2):
            for core, arrays in ((tp, ring), (1 - tp, other)):
                begin = pl.multiple_of(source * block + core * (2 * chunk) + chain * chunk, chunk)
                places.append(
                    (arrays[(steps - 1) * 2 + chain], rows_in.at[pl.ds(begin, chunk)])
                )
    for steps in range(count):
        source = (ctx - steps + count) % count
        for core, arrays in ((tp, heads), (1 - tp, other_heads)):
            begin = pl.multiple_of((core * count + source) * HD, HD)
            places.append((arrays[steps], attended.at[:, pl.ds(begin, HD)]))
        for piece in range(4):
            for core, arrays in ((tp, weights), (1 - tp, other_weights)):
                begin = plane_owner(dp, core, piece) * count + source
                places.append(
                    (
                        arrays[piece].at[steps, pl.ds(0, head_rows)],
                        w_all.at[
                            pl.ds(pl.multiple_of(core * head_rows, head_rows), head_rows),
                            pl.ds(pl.multiple_of(begin * lanes, lanes), lanes),
                        ],
                    )
                )
            begin = pl.multiple_of((plane_owner(dp, tp, piece) * count + source) * local, local)
            for part in range(cols // lanes):
                places.append(
                    (
                        weights[piece].at[steps, pl.ds(head_rows + part * local, local)],
                        w_cross.at[pl.ds(begin, local), pl.ds(part * lanes, lanes)],
                    )
                )
    run_copies(
        [pltpu.make_async_copy(a, b, sem.at[i]) for i, (a, b) in enumerate(places)]
    )
    gains = gain[...]

    @pl.loop(0, user_rows // block)
    def _(slot):
        row_block = order[0, slot]
        here = pl.ds(pl.multiple_of(row_block * block, block), block)
        summed = jnp.dot(attended[here, :], w_all[...], preferred_element_type=jnp.float32)
        coded = (rows_in[here, :].astype(jnp.float32) + summed).astype(jnp.bfloat16)

        @pl.when(row_block == ctx)
        def _():
            encoded[0] = coded

        final = rms_norm(coded, gains).astype(jnp.bfloat16)
        made = jnp.dot(final, w_cross[...], preferred_element_type=jnp.float32)
        made_all[pl.ds(pl.multiple_of(slot * block, block), block), :] = made.astype(jnp.bfloat16)

    out[0, 0] = made_all[...].T


def head_per_device(
    tokens,
    lengths,
    block_order,
    norm_gain,
    w_query,
    w_key,
    w_value,
    w_out,
    final_gain,
    w_cross_key,
    w_cross_value,
):
    _, block, width = tokens.shape
    count = lax.axis_size("ctx")
    local, head_cols = w_query.shape
    head_rows, lanes = w_out.shape
    user_rows = count * block
    chunk = block // 4
    cols = 2 * head_cols // count
    bf16 = jnp.bfloat16
    whole = pl.BlockSpec(memory_space=pltpu.VMEM)
    scalars = pl.BlockSpec(memory_space=pltpu.SMEM)

    core = lax.axis_index("tp")
    ring_order = line_ring(count)
    ring_pairs = [(ring_order[i], ring_order[(i + 1) % count]) for i in range(count)]
    chains = [
        lax.dynamic_slice_in_dim(tokens[0], core * (2 * chunk) + chain * chunk, chunk, 0)
        for chain in range(2)
    ]
    pieces = pl.pallas_call(
        functools.partial(split_self, count),
        out_shape=[jax.ShapeDtypeStruct((local, 3 * HD), bf16)] * count,
        in_specs=[whole] * 3,
        out_specs=[whole] * count,
        name="split_self",
    )(w_query, w_key, w_value)
    moved = [pieces[0]] + [shift_over(pieces[s], "ctx", s) for s in range(1, count)]
    self_weights = gather_plane(jnp.stack(moved))

    ring, other = [], []
    for _ in range(count - 1):
        chains = [lax.ppermute(one, "ctx", ring_pairs) for one in chains]
        ring += chains
        other += [swap_cores(one) for one in chains]

    n_ring = len(ring)
    n_copies = 1 + 2 * n_ring + 4 * count
    attended = pl.pallas_call(
        functools.partial(attend_kernel, count, (user_rows, block, chunk, local)),
        out_shape=jax.ShapeDtypeStruct((user_rows, HD), bf16),
        in_specs=[scalars, whole] + any_specs(1 + 2 * n_ring + 4),
        out_specs=whole,
        scratch_shapes=[
            pltpu.VMEM((user_rows, width), bf16),
            pltpu.VMEM((width, 3 * HD), bf16),
            pltpu.VMEM((user_rows, 3 * HD), bf16),
            pltpu.SemaphoreType.DMA((n_copies,)),
        ],
        cost_estimate=pl.CostEstimate(
            flops=2 * user_rows * width * 3 * HD + 4 * user_rows * user_rows * HD,
            bytes_accessed=2 * (user_rows * width + width * 3 * HD + user_rows * HD),
            transcendentals=user_rows * user_rows,
        ),
        name="attend",
    )(lengths, norm_gain[None], tokens, *ring, *other, *self_weights)

    w_out, w_cross_key, w_cross_value, _ = lax.optimization_barrier(
        (w_out, w_cross_key, w_cross_value, ring[-1])
    )
    piece_rows = head_rows + cols // lanes * local
    pieces = pl.pallas_call(
        functools.partial(split_cross, count),
        out_shape=[jax.ShapeDtypeStruct((piece_rows, lanes), bf16)] * count,
        in_specs=[whole] * 3,
        out_specs=[whole] * count,
        name="split_cross",
    )(w_out, w_cross_key, w_cross_value)
    moved = [pieces[0]] + [shift_over(pieces[s], "ctx", s) for s in range(1, count)]
    weights = gather_plane(jnp.stack(moved))
    other_weights = [swap_cores(one) for one in weights]

    heads = [attended] + [shift_over(attended, "ctx", s) for s in range(1, count)]
    other_heads = [swap_cores(one) for one in heads]

    n_copies = 1 + 2 * n_ring + count * (2 + 4 * (2 + cols // lanes))
    encoded, crossed = pl.pallas_call(
        functools.partial(
            finish_kernel, count, (user_rows, block, chunk, local, head_rows, lanes, cols)
        ),
        out_shape=[
            jax.ShapeDtypeStruct(tokens.shape, bf16),
            jax.ShapeDtypeStruct((1, 1, cols, user_rows), bf16),
        ],
        in_specs=[scalars, whole] + any_specs(1 + 2 * n_ring + 2 * count + 8),
        out_specs=[whole, whole],
        scratch_shapes=[
            pltpu.VMEM((user_rows, width), bf16),
            pltpu.VMEM((user_rows, 2 * head_rows), bf16),
            pltpu.VMEM((2 * head_rows, width), bf16),
            pltpu.VMEM((width, cols), bf16),
            pltpu.VMEM((user_rows, cols), bf16),
            pltpu.SemaphoreType.DMA((n_copies,)),
        ],
        cost_estimate=pl.CostEstimate(
            flops=2 * user_rows * width * (2 * head_rows + cols),
            bytes_accessed=2 * (2 * user_rows * width + 2 * head_rows * width + width * cols),
            transcendentals=0,
        ),
        name="finish",
    )(block_order, final_gain[None], tokens, *ring, *other, *heads, *other_heads, *weights, *other_weights)
    return (encoded, crossed)


def per_device(*arrays):
    tokens, w_query, w_out = arrays[0], arrays[4], arrays[7]
    dp_count, ctx_count, tp_count = (lax.axis_size(name) for name in ("dp", "ctx", "tp"))
    fits = (
        tp_count == 2
        and dp_count == 4
        and ctx_count % 2 == 0
        and w_query.shape[1] == ctx_count * HD
        and tokens.shape[0] == 1
        and tokens.shape[1] % 64 == 0
        and w_query.shape[0] % 128 == 0
        and w_out.shape[1] == 128
    )
    return (head_per_device if fits else gathered_weights)(*arrays)


def solution(mesh):
    placed = (
        P("dp", "ctx", None),
        P("dp"),
        P("dp", None),
        P(),
        P(("dp", "ctx"), "tp"),
        P(("dp", "ctx"), "tp"),
        P(("dp", "ctx"), "tp"),
        P("tp", ("dp", "ctx")),
        P(),
        P(("dp", "ctx"), "tp"),
        P(("dp", "ctx"), "tp"),
    )
    return jax.shard_map(
        per_device,
        mesh=mesh,
        in_specs=placed,
        out_specs=(P("dp", "ctx", None), P("dp", "tp", "ctx", None)),
        check_vma=False,
    )
```
